256 devices in a mesh: cuts: 4 (over x), lat: 64 (over y, z, core).
Axes of the slice: x: 4, y: 4, z: 8, core: 2. Of those that a mesh axis runs over, the one named last changes fastest.
Arguments:
- object_contrast: float32 [2, 4, 8192, 4096], P(None, 'cuts', 'lat'), may hold values from -0.9 to 0.9
- probe: float32 [2, 256, 256], replicated, may hold values from -4.2 to 4.2
- intensity: float32 [256, 256, 256], P('lat'), may hold values from 0 to 3
- positions: int32 [256, 2], P('lat'), may hold values from -128 to 8064, as said below
- counts: int32 [64], P('lat'), may hold values from 1 to 4, as said below
Outputs:
- gradient: float32 [2, 4, 8192, 4096], P(None, 'cuts', 'lat')
The draws below stay inside these ranges and needn't reach their ends.
Inputs may be any that keep to these rules, and one draw needn't show every extreme that they name: `positions`: position p = o * 4 + j belongs to lateral owner o. Its first entry is a multiple of 8 from (o - 1) * 128 to o * 128; its second entry is a multiple of 128 from 0 to 3840. Slots o * 4 + j with j >= counts[o] are unused. Owner 0 has 4 live positions in every draw.
All inputs are finite; a program needn't handle non-finite values.
Results may differ from the reference program's by a relative error of at most 0.0003.
Values sent between devices are 32-bit elements; how exact they have to be, the bound alone decides.
No kernel may reach another device: no remote copies, remote signals or barrier semaphores. Data moves between devices by JAX's collectives and lax.ppermute only.
A program may use at most 128 MiB of HBM per device.

```python
import math
import jax
import jax.numpy as jnp
from jax import lax

PATCH = 256
W = 4096
P_CAP = 4
STRIP = 128
OWNERS = 64
NY = 8192
SLICES = 4
POSITIONS = 256


def draw_counts(key, part):
    lower = jax.random.randint(jax.random.fold_in(key, 11), (OWNERS,), 1, P_CAP // 2 + 1)
    busiest = jax.random.randint(jax.random.fold_in(key, 12), (OWNERS // 16 + 1,), 0, OWNERS)
    return lower.at[busiest].set(P_CAP).at[0].set(P_CAP).astype(jnp.int32)


def draw_positions(key, part):
    owner = jnp.arange(POSITIONS, dtype=jnp.int32) // P_CAP
    row_steps = jax.random.randint(jax.random.fold_in(key, 21), (POSITIONS,), 0, STRIP // 8 + 1)
    first_rows = (owner - 1) * STRIP + row_steps * 8
    col_steps = jax.random.randint(jax.random.fold_in(key, 22), (POSITIONS,), 0, (W - PATCH) // (PATCH // 2) + 1)
    first_cols = col_steps * (PATCH // 2)
    first_rows = first_rows.at[0].set(-STRIP).at[1].set(0).at[(OWNERS - 1) * P_CAP].set((OWNERS - 1) * STRIP)
    first_cols = first_cols.at[0].set(W - PATCH).at[1].set(0)
    return jnp.stack([first_rows, first_cols], axis=1).astype(jnp.int32)


def block_scale(key, dims, split, smallest, largest):
    level, own = 1.0, jax.random.fold_in(key, 6)
    for axis_at, shards_of in split:
        draws = jnp.exp(jax.random.uniform(jax.random.fold_in(own, axis_at), (shards_of,), jnp.float32, smallest / len(split), largest / len(split)))
        level = level * jnp.repeat(draws, dims[axis_at] // shards_of).reshape([-1 if axis == axis_at else 1 for axis in range(len(dims))])
    return level


def normal_values(stream_key, dims, spread, limit, cuts=(), held_as=jnp.bfloat16):
    values = spread * jax.random.normal(stream_key, dims, jnp.float32)
    if cuts:
        values = values * block_scale(stream_key, dims, cuts, -0.22, 0.18)
    return jnp.clip(values, -limit, limit).astype(held_as)


def setup_inputs(seed: int = 0) -> dict:
    splits = jax.random.split(jax.random.key(seed), 6)
    object_contrast = normal_values(splits[0], (2, SLICES, NY, W), 0.15, 0.9, ((1, 4), (2, 64)), jnp.float32)
    probe = normal_values(splits[1], (2, PATCH, PATCH), 0.7, 4.2, (), jnp.float32)
    intensity = jnp.clip(3.0 * jax.random.uniform(splits[2], (POSITIONS, PATCH, PATCH), jnp.float32) ** block_scale(splits[2], (POSITIONS, PATCH, PATCH), ((0, 64),), -0.2, 0.2), 0.0, 3.0)
    positions = draw_positions(jax.random.fold_in(splits[5], 71), 0)
    counts = draw_counts(jax.random.fold_in(splits[5], 71), 0)
    return {"object_contrast": object_contrast, "probe": probe, "intensity": intensity, "positions": positions, "counts": counts}


PHASE_COEF = 64.0 * math.pi


def kernel_parts(patch_size):
    ticks = jnp.arange(patch_size, dtype=jnp.int32)
    freqs = jnp.where(ticks < patch_size // 2, ticks, ticks - patch_size).astype(jnp.float32)
    phase = PHASE_COEF * (freqs[:, None] * freqs[:, None] + freqs[None, :] * freqs[None, :]) / (patch_size * patch_size)
    return jnp.cos(phase), -jnp.sin(phase)


def forward_dft(field):
    return jnp.fft.fft2(field, norm="ortho")


def inverse_dft(field):
    return jnp.fft.ifft2(field, norm="ortho")


def position_gradient(window, probe_wave, measured, kernel):
    transmit = 1.0 + lax.complex(window[0], window[1])
    wavefield = probe_wave
    stored = []
    shaped = wavefield
    for slice_index in range(SLICES):
        stored.append(wavefield)
        shaped = transmit[slice_index] * wavefield
        if slice_index < SLICES - 1:
            wavefield = inverse_dft(kernel * forward_dft(shaped))
    detector = forward_dft(shaped)
    squared = jnp.real(detector) ** 2 + jnp.imag(detector) ** 2
    adjoint = inverse_dft((squared - measured) * detector)
    pieces = [None] * SLICES
    for slice_index in range(SLICES - 1, -1, -1):
        pieces[slice_index] = jnp.conj(stored[slice_index]) * adjoint
        if slice_index > 0:
            adjoint = inverse_dft(jnp.conj(kernel) * forward_dft(jnp.conj(transmit[slice_index]) * adjoint))
    stacked = jnp.stack(pieces)
    return jnp.stack([jnp.real(stacked), jnp.imag(stacked)])


def reference(object_contrast, probe, intensity, positions, counts):
    patch_size = PATCH
    real_kernel, imag_kernel = kernel_parts(patch_size)
    kernel = lax.complex(real_kernel, imag_kernel)
    probe_wave = lax.complex(probe[0], probe[1])
    padded = jnp.pad(object_contrast, ((0, 0), (0, 0), (STRIP, STRIP), (0, 0)))
    slot_ids = jnp.arange(POSITIONS, dtype=jnp.int32)
    alive = (slot_ids % P_CAP) < counts[slot_ids // P_CAP]

    def add_position(summed, item):
        place, measured, live_flag = item
        anchor = jnp.zeros((), jnp.int32)
        first_row = (place[0] + STRIP).astype(jnp.int32)
        first_col = place[1].astype(jnp.int32)
        start = (anchor, anchor, first_row, first_col)
        window = lax.dynamic_slice(padded, start, (2, SLICES, patch_size, patch_size))
        contribution = position_gradient(window, probe_wave, measured, kernel)
        contribution = jnp.where(live_flag, contribution, jnp.zeros_like(contribution))
        current = lax.dynamic_slice(summed, start, (2, SLICES, patch_size, patch_size))
        return lax.dynamic_update_slice(summed, current + contribution, start), None

    summed, _ = lax.scan(add_position, jnp.zeros_like(padded), (positions, intensity, alive))
    return summed[:, :, STRIP:STRIP + NY]
```

```python
import math

import jax
import jax.numpy as jnp
import numpy as np
from jax import lax
from jax.experimental import pallas as pl
from jax.experimental.pallas import tpu as pltpu
from jax.sharding import PartitionSpec as P

PHASE_COEF = 64.0 * math.pi
VMEM = pl.BlockSpec(memory_space=pltpu.VMEM)
SMEM = pl.BlockSpec(memory_space=pltpu.SMEM)
ANY = pl.BlockSpec(memory_space=pl.ANY)


def split_table(table):
    high = table.astype(jnp.bfloat16)
    low = (table - high.astype(np.float64)).astype(jnp.bfloat16)
    return [high, low]


def wave_tables(size):
    ticks = np.arange(size)
    freqs = np.where(ticks < size // 2, ticks, ticks - size).astype(np.float64)
    turns = (ticks[:, None] * ticks[None, :]) % size
    fourier = np.exp(-2j * np.pi * turns / size) / math.sqrt(size)
    axis_kernel = np.exp(-1j * PHASE_COEF * freqs * freqs / (size * size))
    spread = np.conj(fourier) @ (axis_kernel[:, None] * fourier)
    parts = []
    for table in (spread, fourier):
        parts += split_table(table.real) + split_table(table.imag)
    return np.stack(parts)


def cut_slabs(object_slab, columns, width):
    count = columns.shape[0]
    planes, rows, _ = object_slab.shape

    def body(columns_ref, slab_ref, out_ref, sems):
        def copy(k):
            start = pl.multiple_of(columns_ref[k], 128)
            return pltpu.make_async_copy(
                slab_ref.at[:, :, pl.ds(start, width)], out_ref.at[k], sems.at[k]
            )

        for k in range(count):
            copy(k).start()
        for k in range(count):
            copy(k).wait()

    return pl.pallas_call(
        body,
        out_shape=jax.ShapeDtypeStruct((count, planes, rows, width), jnp.float32),
        in_specs=[SMEM, ANY],
        out_specs=VMEM,
        scratch_shapes=[pltpu.SemaphoreType.DMA((count,))],
        name="cut_slabs",
    )(columns, object_slab)


def chain(control, own, halo, probe, intensity, tables):
    slices, _, strip, size = own.shape
    half = jnp.bfloat16

    def body(control_ref, own_ref, halo_ref, probe_ref, intensity_ref, tables_ref, grad_own, grad_halo,
             twice, waves, left_a, right_a, left_f, right_f, stack, rows, measured, sem):
        live = control_ref[0]
        slot = control_ref[1]
        shift = pl.multiple_of(control_ref[2], 8)

        @pl.when(live == 0)
        def _():
            grad_own[...] = jnp.zeros_like(grad_own)
            grad_halo[...] = jnp.zeros_like(grad_halo)

        def split(value):
            high = value.astype(half)
            return high, (value - high.astype(jnp.float32)).astype(half)

        def put_left(base, count, real, imag):
            for offset, value in ((0, real), (size, imag)):
                high, low = split(value)
                stack[pl.ds(offset + base, count), :] = high
                stack[pl.ds(2 * size + offset + base, count), :] = high
                stack[pl.ds(4 * size + offset + base, count), :] = low

        def sandwich(left, right):
            middle = jnp.dot(left[...], stack[...], preferred_element_type=jnp.float32)
            for part in range(2):
                high, low = split(middle[part * size : (part + 1) * size])
                rows[:, part * size : (part + 1) * size] = high
                rows[:, (2 + part) * size : (3 + part) * size] = high
                rows[:, (4 + part) * size : (5 + part) * size] = low
            return jnp.dot(rows[...], right[...], preferred_element_type=jnp.float32)

        def modulate(index, real, imag):
            for base, ref in ((0, own_ref), (strip, halo_ref)):
                t_real = 1.0 + ref[index, 0]
                t_imag = ref[index, 1]
                v_real = real[base : base + strip]
                v_imag = imag[base : base + strip]
                put_left(base, strip, t_real * v_real - t_imag * v_imag, t_real * v_imag + t_imag * v_real)

        def emit(index, real, imag):
            w_real = waves[index, 0]
            w_imag = waves[index, 1]
            g_real = w_real * real - w_imag * imag
            g_imag = -(w_real * imag + w_imag * real)
            grad_own[index, 0] = g_real[:strip]
            grad_own[index, 1] = g_imag[:strip]
            grad_halo[index, 0] = g_real[strip:]
            grad_halo[index, 1] = g_imag[strip:]

        @pl.when(live != 0)
        def _():
            fetch = pltpu.make_async_copy(intensity_ref.at[slot], measured, sem)
            fetch.start()
            for base, left, right in ((0, left_a, right_a), (4, left_f, right_f)):
                for place, low in ((0, 0), (1, 1), (2, 0)):
                    real = tables_ref[base + low]
                    imag = tables_ref[base + 2 + low]
                    at = 2 * size * place
                    left[:size, at : at + size] = real
                    left[:size, at + size : at + 2 * size] = -imag
                    left[size:, at : at + size] = imag
                    left[size:, at + size : at + 2 * size] = real
                    right[at : at + size, :size] = real
                    right[at : at + size, size:] = imag
                    right[at + size : at + 2 * size, :size] = -imag
                    right[at + size : at + 2 * size, size:] = real
            twice[:, :size] = probe_ref[...]
            twice[:, size:] = probe_ref[...]
            waves[0] = twice[:, pl.ds(shift, size), :]

            @pl.loop(0, slices - 1)
            def _(index):
                modulate(index, waves[index, 0], waves[index, 1])
                out = sandwich(left_a, right_a)
                waves[index + 1, 0] = out[:, :size]
                waves[index + 1, 1] = out[:, size:]

            modulate(slices - 1, waves[slices - 1, 0], waves[slices - 1, 1])
            far = sandwich(left_f, right_f)
            far_real = far[:, :size]
            far_imag = far[:, size:]
            fetch.wait()
            misfit = far_real * far_real + far_imag * far_imag - measured[...]
            put_left(0, size, misfit * far_real, -misfit * far_imag)
            back = sandwich(left_f, right_f)
            emit(slices - 1, back[:, :size], back[:, size:])
            twice[:, :size] = jnp.stack([back[:, :size], back[:, size:]])

            @pl.loop(0, slices - 1)
            def _(step):
                index = slices - 1 - step
                modulate(index, twice[0, :size], twice[1, :size])
                out = sandwich(left_a, right_a)
                emit(index - 1, out[:, :size], out[:, size:])
                twice[0, :size] = out[:, :size]
                twice[1, :size] = out[:, size:]

    return pl.pallas_call(
        body,
        out_shape=[jax.ShapeDtypeStruct(own.shape, jnp.float32)] * 2,
        in_specs=[SMEM, VMEM, VMEM, VMEM, ANY, VMEM],
        out_specs=[VMEM, VMEM],
        scratch_shapes=[
            pltpu.VMEM((2, 2 * size, size), jnp.float32),
            pltpu.VMEM((slices, 2, size, size), jnp.float32),
            pltpu.VMEM((2 * size, 6 * size), half),
            pltpu.VMEM((6 * size, 2 * size), half),
            pltpu.VMEM((2 * size, 6 * size), half),
            pltpu.VMEM((6 * size, 2 * size), half),
            pltpu.VMEM((6 * size, size), half),
            pltpu.VMEM((size, 6 * size), half),
            pltpu.VMEM((size, size), jnp.float32),
            pltpu.SemaphoreType.DMA,
        ],
        name="chain",
    )(control, own, halo, probe, intensity, tables)


def gather_strip(places, own, from_above, from_below, width):
    count, planes, strip, size = own.shape
    block = 16

    def body(places_ref, own_ref, above_ref, below_ref, out_ref):
        first = pl.program_id(0) * block
        row = lax.broadcasted_iota(jnp.int32, (planes, block, size), 1) + first
        out_ref[...] = jnp.zeros_like(out_ref)
        for group, ref in enumerate((own_ref, above_ref, below_ref)):
            for k in range(count):
                start = pl.multiple_of(places_ref[group, k, 1], 128)
                edge = places_ref[group, k, 0]
                value = ref[k]
                if group == 1:
                    value = jnp.where(row < edge, value, 0.0)
                if group == 2:
                    value = jnp.where(row >= edge, value, 0.0)
                at = (slice(None), slice(None), pl.ds(start, size))
                out_ref[at] = out_ref[at] + value

    spec = pl.BlockSpec((count, planes, block, size), lambda i: (0, 0, i, 0))
    return pl.pallas_call(
        body,
        grid=(strip // block,),
        out_shape=jax.ShapeDtypeStruct((planes, strip, width), jnp.float32),
        in_specs=[SMEM, spec, spec, spec],
        out_specs=pl.BlockSpec((planes, block, width), lambda i: (0, i, 0)),
        name="gather_strip",
    )(places, own, from_above, from_below)


def on_device(object_contrast, probe, intensity, positions, counts):
    object_slab = object_contrast[:, 0]
    strip = object_slab.shape[1]
    width = object_slab.shape[2]
    size = probe.shape[-1]
    owner = lax.axis_index("lat")
    slot = lax.axis_index("cuts")
    owners = lax.axis_size("lat")
    downward = [(i, i + 1) for i in range(owners - 1)]
    upward = [(i + 1, i) for i in range(owners - 1)]
    tables = jnp.asarray(wave_tables(size))

    edges = positions[:, 0] - (owner - 1) * strip
    places = jnp.stack([edges, positions[:, 1]], axis=1)
    places_above = lax.ppermute(places, "lat", downward)
    places_below = lax.ppermute(places, "lat", upward)

    own = cut_slabs(object_slab, positions[:, 1], size)
    rim = cut_slabs(
        object_slab, jnp.concatenate([places_above[:, 1], places_below[:, 1]]), size
    )
    slots = positions.shape[0]
    from_below = lax.ppermute(rim[:slots], "lat", upward)
    from_above = lax.ppermute(rim[slots:], "lat", downward)
    own = lax.all_to_all(own, "cuts", 0, 0, tiled=True)
    row = lax.broadcasted_iota(jnp.int32, from_below.shape, 2)
    halo = jnp.where(row < edges[:, None, None, None], from_below, from_above)
    halo = lax.all_to_all(halo, "cuts", 0, 0, tiled=True)

    live = (slot < counts[0]).astype(jnp.int32)
    shift = strip - edges[slot]
    control = jnp.stack([live, slot, shift])
    grad_own, grad_halo = chain(control, own, halo, probe, intensity, tables)

    grad_halo = lax.all_to_all(grad_halo, "cuts", 0, 0, tiled=True)
    back_above = lax.ppermute(grad_halo, "lat", downward)
    back_below = lax.ppermute(grad_halo, "lat", upward)
    grad_own = lax.all_to_all(grad_own, "cuts", 0, 0, tiled=True)
    summed = gather_strip(
        jnp.stack([places, places_above, places_below]), grad_own, back_above, back_below, width
    )
    return summed[:, None]


def solution(mesh):
    return jax.shard_map(
        on_device,
        mesh=mesh,
        in_specs=(
            P(None, "cuts", "lat", None),
            P(),
            P("lat", None, None),
            P("lat", None),
            P("lat"),
        ),
        out_specs=P(None, "cuts", "lat", None),
        check_vma=False,
    )
```

```python
import math

import jax
import jax.numpy as jnp
import numpy as np
from jax import lax
from jax.experimental import pallas as pl
from jax.experimental.pallas import tpu as pltpu
from jax.sharding import PartitionSpec as P

PHASE_COEF = 64.0 * math.pi
VMEM = pl.BlockSpec(memory_space=pltpu.VMEM)
SMEM = pl.BlockSpec(memory_space=pltpu.SMEM)
HBM = pl.BlockSpec(memory_space=pltpu.HBM)
SMALL = pltpu.CompilerParams(vmem_limit_bytes=16 * 1024 * 1024)


def on_chip(shape, dtype=jnp.float32):
    return pltpu.VMEM(shape, dtype)


def chip(value):
    return pltpu.with_memory_space_constraint(value, pltpu.VMEM)


def off_chip(value):
    return pltpu.with_memory_space_constraint(value, pltpu.HBM)


def wave_tables(size):
    half = size // 2
    ticks = np.arange(size)
    freqs = np.where(ticks < half, ticks, ticks - size).astype(np.float64)
    turns = (ticks[:, None] * ticks[None, :]) % size
    fourier = np.exp(-2j * np.pi * turns / size) / math.sqrt(size)
    axis_kernel = np.exp(-1j * PHASE_COEF * freqs * freqs / (size * size))
    spread = np.conj(fourier) @ (axis_kernel[:, None] * fourier)
    near = spread[:half, :half]
    across = spread[:half, half:]
    even = fourier[0::2, :half]
    odd = fourier[1::2, :half]
    parts = []
    for table in ((near + across) / 2, (near - across) / 2, even, odd, odd.T):
        for value in (table.real, table.imag):
            high = value.astype(jnp.bfloat16)
            parts += [high, (value - high.astype(np.float64)).astype(jnp.bfloat16)]
    return np.stack(parts).reshape(5, 4, half, half)


def cut_slabs(object_slab, columns, width):
    count = columns.shape[0]
    planes, rows, _ = object_slab.shape

    def body(columns_ref, slab_ref, out_ref, sems):
        def copy(k):
            start = pl.multiple_of(columns_ref[k], 128)
            return pltpu.make_async_copy(
                slab_ref.at[:, :, pl.ds(start, width)], out_ref.at[k], sems.at[k]
            )

        for k in range(count):
            copy(k).start()
        for k in range(count):
            copy(k).wait()

    return pl.pallas_call(
        body,
        out_shape=on_chip((count, planes, rows, width)),
        in_specs=[SMEM, HBM],
        out_specs=VMEM,
        scratch_shapes=[pltpu.SemaphoreType.DMA((count,))],
        compiler_params=SMALL,
        name="cut_slabs",
    )(columns, off_chip(object_slab))


def split(value):
    high = value.astype(jnp.bfloat16)
    return high, (value - high.astype(jnp.float32)).astype(jnp.bfloat16)


def prepare(control, probe, intensity, tables):
    size = probe.shape[-1]
    half = size // 2
    kinds = tables.shape[0]

    def body(control_ref, probe_ref, intensity_ref, tables_ref, left, right, start, sorted_ref, twice, sort_rows, measured, sems):
        slot = control_ref[1]
        shift = pl.multiple_of(control_ref[2], 8)
        fetches = [
            pltpu.make_async_copy(
                intensity_ref.at[slot, :, column * half : (column + 1) * half], measured.at[column], sems.at[column]
            )
            for column in range(2)
        ]
        for fetch in fetches:
            fetch.start()
        twice[:, :size] = probe_ref[...]
        twice[:, size:] = probe_ref[...]
        start[...] = twice[:, pl.ds(shift, size), :]

        @pl.loop(0, kinds)
        def _(kind):
            for place, low in ((0, 0), (1, 1), (2, 0)):
                real = tables_ref[kind, low]
                imag = tables_ref[kind, 2 + low]
                at = size * place
                left[kind, :half, at : at + half] = real
                left[kind, :half, at + half : at + size] = -imag
                left[kind, half:, at : at + half] = imag
                left[kind, half:, at + half : at + size] = real
                right[kind, at : at + half, :half] = real
                right[kind, at : at + half, half:] = imag
                right[kind, at + half : at + size, :half] = -imag
                right[kind, at + half : at + size, half:] = real

        for fetch in fetches:
            fetch.wait()
        source = lax.broadcasted_iota(jnp.int32, (size, size), 0)
        target = lax.broadcasted_iota(jnp.int32, (size, size), 1)
        picked = jnp.where(target < half, 2 * target, 2 * (target - half) + 1)
        sort_rows[...] = (source == picked).astype(jnp.float32).astype(jnp.bfloat16)
        for part in range(2):
            value = jnp.concatenate(
                [measured[column, pl.ds(part, half, stride=2), :] for column in range(2)], axis=1
            )
            total = None
            for _ in range(3):
                high = value.astype(jnp.bfloat16)
                value = value - high.astype(jnp.float32)
                term = jnp.dot(high, sort_rows[...], preferred_element_type=jnp.float32)
                total = term if total is None else total + term
            sorted_ref[part * half : (part + 1) * half] = total

    return pl.pallas_call(
        body,
        out_shape=[
            jax.ShapeDtypeStruct((kinds, size, 3 * size), jnp.bfloat16),
            jax.ShapeDtypeStruct((kinds, 3 * size, size), jnp.bfloat16),
            jax.ShapeDtypeStruct((2, size, size), jnp.float32),
            jax.ShapeDtypeStruct((size, size), jnp.float32),
        ],
        in_specs=[SMEM, VMEM, HBM, VMEM],
        out_specs=[VMEM] * 4,
        scratch_shapes=[
            pltpu.VMEM((2, 2 * size, size), jnp.float32),
            pltpu.VMEM((size, size), jnp.bfloat16),
            pltpu.VMEM((2, size, half), jnp.float32),
            pltpu.SemaphoreType.DMA((2,)),
        ],
        compiler_params=SMALL,
        name="prepare",
    )(control, probe, off_chip(intensity), tables)


def chain(control, own, halo, left, right, start, measured):
    slices, _, half, size = own.shape
    low_part = jnp.bfloat16

    def body(control_ref, own_ref, halo_ref, left_hbm, right_hbm, start_hbm, measured_hbm, grad_own, grad_halo,
             waves, adjoint, stack, rows, left_ref, right_ref, measured_ref, sems):
        live = control_ref[0]
        near = pl.ds(0, 2)
        rest = pl.ds(2, left_hbm.shape[0] - 2)
        first = [
            pltpu.make_async_copy(start_hbm, waves.at[0], sems.at[0]),
            pltpu.make_async_copy(left_hbm.at[near], left_ref.at[near], sems.at[1]),
            pltpu.make_async_copy(right_hbm.at[near], right_ref.at[near], sems.at[2]),
        ]
        later = [
            pltpu.make_async_copy(left_hbm.at[rest], left_ref.at[rest], sems.at[3]),
            pltpu.make_async_copy(right_hbm.at[rest], right_ref.at[rest], sems.at[4]),
            pltpu.make_async_copy(measured_hbm, measured_ref, sems.at[5]),
        ]

        @pl.when(live == 0)
        def _():
            grad_own[...] = jnp.zeros_like(grad_own)
            grad_halo[...] = jnp.zeros_like(grad_halo)

        def put_stack(branch, part, value):
            high, low = split(value)
            at = part * half
            stack[branch, at : at + half] = high
            stack[branch, size + at : size + at + half] = high
            stack[branch, 2 * size + at : 2 * size + at + half] = low

        def put_rows(branch, block, part, value):
            high, low = split(value)
            at = part * half
            here = slice(block * half, (block + 1) * half)
            rows[branch, here, at : at + half] = high
            rows[branch, here, size + at : size + at + half] = high
            rows[branch, here, 2 * size + at : 2 * size + at + half] = low

        def sandwich(left_kinds, right_kinds, mix):
            for block in range(2):
                middle = jnp.dot(
                    left_ref[left_kinds[block]], stack[block], preferred_element_type=jnp.float32
                )
                for part in range(2):
                    one = middle[part * half : (part + 1) * half, :half]
                    two = middle[part * half : (part + 1) * half, half:]
                    put_rows(0, block, part, one + two if mix else one)
                    put_rows(1, block, part, one - two if mix else two)
            return [
                jnp.dot(rows[branch], right_ref[right_kinds[branch]], preferred_element_type=jnp.float32)
                for branch in range(2)
            ]

        def unmix(first, second, put):
            for column, side in ((0, first + second), (1, first - second)):
                for part in range(2):
                    one = side[:half, part * half : (part + 1) * half]
                    two = side[half:, part * half : (part + 1) * half]
                    put(part, 0, column, one + two)
                    put(part, 1, column, one - two)

        def modulate(index, source, at):
            values = []
            for ref, base in ((own_ref, 0), (halo_ref, half)):
                t_real = 1.0 + ref[index, 0]
                t_imag = ref[index, 1]
                v_real = source[at, 0, base : base + half]
                v_imag = source[at, 1, base : base + half]
                values.append((t_real * v_real - t_imag * v_imag, t_real * v_imag + t_imag * v_real))
            (top_real, top_imag), (low_real, low_imag) = values
            put_stack(0, 0, top_real + low_real)
            put_stack(0, 1, top_imag + low_imag)
            put_stack(1, 0, top_real - low_real)
            put_stack(1, 1, top_imag - low_imag)

        def keep(target, at):
            def put(part, row, column, value):
                target[at, part, row * half : (row + 1) * half, column * half : (column + 1) * half] = value

            return put

        def emit(index):
            for base, target in ((0, grad_own), (half, grad_halo)):
                w_real = waves[index, 0, base : base + half]
                w_imag = waves[index, 1, base : base + half]
                a_real = adjoint[0, 0, base : base + half]
                a_imag = adjoint[0, 1, base : base + half]
                target[index, 0] = w_real * a_real - w_imag * a_imag
                target[index, 1] = -(w_real * a_imag + w_imag * a_real)

        @pl.when(live != 0)
        def _():
            for copy in first + later:
                copy.start()
            for copy in first:
                copy.wait()

            @pl.loop(0, slices - 1)
            def _(index):
                modulate(index, waves, index)
                unmix(*sandwich((0, 1), (0, 1), True), keep(waves, index + 1))

            modulate(slices - 1, waves, slices - 1)
            for copy in later:
                copy.wait()
            for column, far in enumerate(sandwich((2, 3), (2, 4), True)):
                across = slice(column * half, (column + 1) * half)
                for block in range(2):
                    here = slice(block * half, (block + 1) * half)
                    far_real = far[here, :half]
                    far_imag = far[here, half:]
                    misfit = far_real * far_real + far_imag * far_imag - measured_ref[here, across]
                    for part, value in ((0, misfit * far_real), (1, -misfit * far_imag)):
                        high, low = split(value)
                        at = part * half
                        stack[block, at : at + half, across] = high
                        stack[block, size + at : size + at + half, across] = high
                        stack[block, 2 * size + at : 2 * size + at + half, across] = low
            unmix(*sandwich((2, 4), (2, 3), False), keep(adjoint, 0))
            emit(slices - 1)

            @pl.loop(0, slices - 1)
            def _(step):
                index = slices - 1 - step
                modulate(index, adjoint, 0)
                unmix(*sandwich((0, 1), (0, 1), True), keep(adjoint, 0))
                emit(index - 1)

    return pl.pallas_call(
        body,
        out_shape=[on_chip(own.shape)] * 2,
        in_specs=[SMEM, VMEM, VMEM, HBM, HBM, HBM, HBM],
        out_specs=[VMEM, VMEM],
        scratch_shapes=[
            pltpu.VMEM((slices, 2, size, size), jnp.float32),
            pltpu.VMEM((1, 2, size, size), jnp.float32),
            pltpu.VMEM((2, 3 * size, size), low_part),
            pltpu.VMEM((2, size, 3 * size), low_part),
            pltpu.VMEM(left.shape, low_part),
            pltpu.VMEM(right.shape, low_part),
            pltpu.VMEM(measured.shape, jnp.float32),
            pltpu.SemaphoreType.DMA((6,)),
        ],
        compiler_params=SMALL,
        name="chain",
    )(control, chip(own), chip(halo), *[off_chip(value) for value in (left, right, start, measured)])


def gather_strip(places, own, from_above, from_below, width):
    count, planes, strip, size = own.shape
    block = 16
    steps = strip // block

    def body(places_ref, own_ref, above_ref, below_ref, out_ref, total, sems):
        row = lax.broadcasted_iota(jnp.int32, (planes, block, size), 1)

        def copy(step):
            return pltpu.make_async_copy(
                total.at[step % 2], out_ref.at[:, pl.ds(step * block, block)], sems.at[step % 2]
            )

        for step in range(steps):
            here = total.at[step % 2]
            if step >= 2:
                copy(step - 2).wait()
            here[...] = jnp.zeros_like(here)
            for group, ref in enumerate((own_ref, above_ref, below_ref)):
                for k in range(count):
                    start = pl.multiple_of(places_ref[group, k, 1], 128)
                    edge = places_ref[group, k, 0] - step * block
                    value = ref[k, :, step * block : (step + 1) * block]
                    if group == 1:
                        value = jnp.where(row < edge, value, 0.0)
                    if group == 2:
                        value = jnp.where(row >= edge, value, 0.0)
                    at = (slice(None), slice(None), pl.ds(start, size))
                    here[at] = here[at] + value
            copy(step).start()
        copy(steps - 2).wait()
        copy(steps - 1).wait()

    return pl.pallas_call(
        body,
        out_shape=jax.ShapeDtypeStruct((planes, strip, width), jnp.float32),
        in_specs=[SMEM, VMEM, VMEM, VMEM],
        out_specs=HBM,
        scratch_shapes=[
            pltpu.VMEM((2, planes, block, width), jnp.float32),
            pltpu.SemaphoreType.DMA((2,)),
        ],
        compiler_params=SMALL,
        name="gather_strip",
    )(places, chip(own), chip(from_above), chip(from_below))


def on_device(object_contrast, probe, intensity, positions, counts):
    object_slab = object_contrast[:, 0]
    strip = object_slab.shape[1]
    width = object_slab.shape[2]
    size = probe.shape[-1]
    slots = positions.shape[0]
    owner = lax.axis_index("lat")
    slot = lax.axis_index("cuts")
    owners = lax.axis_size("lat")
    downward = [(i, i + 1) for i in range(owners - 1)]
    upward = [(i + 1, i) for i in range(owners - 1)]
    tables = jnp.asarray(wave_tables(size))

    edges = positions[:, 0] - (owner - 1) * strip
    places = jnp.stack([edges, positions[:, 1]], axis=1)
    live = (slot < counts[0]).astype(jnp.int32)
    control = jnp.stack([live, slot, strip - edges[slot]])
    left, right, start, measured = prepare(control, probe, intensity, tables)

    places_above = lax.ppermute(places, "lat", downward)
    places_below = lax.ppermute(places, "lat", upward)
    own = cut_slabs(object_slab, positions[:, 1], size)
    own = lax.all_to_all(own, "cuts", 0, 0, tiled=True)
    for_above = cut_slabs(object_slab, places_above[:, 1], size)
    for_below = cut_slabs(object_slab, places_below[:, 1], size)
    from_below = lax.ppermute(for_above, "lat", upward)
    from_above = lax.ppermute(for_below, "lat", downward)
    row = lax.broadcasted_iota(jnp.int32, from_below.shape, 2)
    halo = jnp.where(row < edges[:, None, None, None], from_below, from_above)
    halo = lax.all_to_all(halo, "cuts", 0, 0, tiled=True)

    grad_own, grad_halo = chain(control, own, halo, left, right, start, measured)

    grad_halo = lax.all_to_all(grad_halo, "cuts", 0, 0, tiled=True)
    back_above = lax.ppermute(grad_halo, "lat", downward)
    back_below = lax.ppermute(grad_halo, "lat", upward)
    grad_own = lax.all_to_all(grad_own, "cuts", 0, 0, tiled=True)
    summed = gather_strip(
        jnp.stack([places, places_above, places_below]), grad_own, back_above, back_below, width
    )
    return summed[:, None]


def solution(mesh):
    return jax.shard_map(
        on_device,
        mesh=mesh,
        in_specs=(
            P(None, "cuts", "lat", None),
            P(),
            P("lat", None, None),
            P("lat", None),
            P("lat"),
        ),
        out_specs=P(None, "cuts", "lat", None),
        check_vma=False,
    )
```

```python
import math

import jax
import jax.numpy as jnp
import numpy as np
from jax import lax
from jax.experimental import pallas as pl
from jax.experimental.pallas import tpu as pltpu
from jax.sharding import PartitionSpec as P


PHASE_COEF = 64.0 * math.pi
VMEM = pl.BlockSpec(memory_space=pltpu.VMEM)
SMEM = pl.BlockSpec(memory_space=pltpu.SMEM)
HBM = pl.BlockSpec(memory_space=pltpu.HBM)
SMALL = pltpu.CompilerParams(vmem_limit_bytes=16 * 1024 * 1024)


def on_chip(shape, dtype=jnp.float32):
    return pltpu.VMEM(shape, dtype)


def chip(value):
    return pltpu.with_memory_space_constraint(value, pltpu.VMEM)


def off_chip(value):
    return pltpu.with_memory_space_constraint(value, pltpu.HBM)


def wave_tables(size):
    half = size // 2
    ticks = np.arange(size)
    freqs = np.where(ticks < half, ticks, ticks - size).astype(np.float64)
    turns = (ticks[:, None] * ticks[None, :]) % size
    fourier = np.exp(-2j * np.pi * turns / size) / math.sqrt(size)
    axis_kernel = np.exp(-1j * PHASE_COEF * freqs * freqs / (size * size))
    spread = np.conj(fourier) @ (axis_kernel[:, None] * fourier)
    near = spread[:half, :half]
    across = spread[:half, half:]
    even = fourier[0::2, :half]
    odd = fourier[1::2, :half]
    parts = []
    for table in ((near + across) / 2, (near - across) / 2, even, odd, odd.T):
        for value in (table.real, table.imag):
            high = value.astype(jnp.bfloat16)
            parts += [high, (value - high.astype(np.float64)).astype(jnp.bfloat16)]
    return np.stack(parts).reshape(5, 4, half, half)


def cut_own(slot, object_slab, columns, width):
    count = columns.shape[0]
    planes, rows, _ = object_slab.shape

    def body(slot_ref, columns_ref, slab_ref, *refs):
        sems = refs[count]
        copies = []
        for k in range(count):
            start = pl.multiple_of(columns_ref[lax.rem(slot_ref[0] + k, count)], 128)
            copies.append(
                pltpu.make_async_copy(slab_ref.at[:, :, pl.ds(start, width)], refs[k], sems.at[k])
            )
        for copy in copies:
            copy.start()
        for copy in copies:
            copy.wait()

    return pl.pallas_call(
        body,
        out_shape=[on_chip((planes, rows, width))] * count,
        in_specs=[SMEM, SMEM, HBM],
        out_specs=[VMEM] * count,
        scratch_shapes=[pltpu.SemaphoreType.DMA((count,))],
        compiler_params=SMALL,
        name="cut_own",
    )(slot, columns, off_chip(object_slab))


def cut_rims(object_slab, above, below, width):
    count = above.shape[0]
    planes, rows, _ = object_slab.shape

    def body(above_ref, below_ref, slab_ref, for_above, for_below, sems):
        copies = []
        for side, (places_ref, target) in enumerate(((above_ref, for_above), (below_ref, for_below))):
            for k in range(count):
                start = pl.multiple_of(places_ref[k, 1], 128)
                copies.append(
                    pltpu.make_async_copy(
                        slab_ref.at[:, :, pl.ds(start, width)], target.at[k], sems.at[side, k]
                    )
                )
        for copy in copies:
            copy.start()
        for copy in copies:
            copy.wait()

    return pl.pallas_call(
        body,
        out_shape=[on_chip((count, planes, rows, width))] * 2,
        in_specs=[SMEM, SMEM, HBM],
        out_specs=[VMEM] * 2,
        scratch_shapes=[pltpu.SemaphoreType.DMA((2, count))],
        compiler_params=SMALL,
        name="cut_rims",
    )(above, below, off_chip(object_slab))


def blend(places, from_above, from_below):
    count, planes, rows, width = from_above.shape

    def body(places_ref, above_ref, below_ref, out_ref):
        row = lax.broadcasted_iota(jnp.int32, (planes, rows, width), 1)
        for k in range(count):
            out_ref[k] = jnp.where(row < places_ref[k, 0], below_ref[k], above_ref[k])

    return pl.pallas_call(
        body,
        out_shape=on_chip(from_above.shape),
        in_specs=[SMEM, VMEM, VMEM],
        out_specs=VMEM,
        compiler_params=SMALL,
        name="blend",
    )(places, chip(from_above), chip(from_below))


def split(value):
    high = value.astype(jnp.bfloat16)
    return high, (value - high.astype(jnp.float32)).astype(jnp.bfloat16)


def prepare(control, probe, intensity, tables):
    size = probe.shape[-1]
    half = size // 2
    kinds = tables.shape[0]

    def body(control_ref, probe_ref, intensity_ref, tables_ref, left, right, start, sorted_ref, twice, sort_rows, measured, sems):
        slot = control_ref[1]
        shift = pl.multiple_of(control_ref[2], 8)
        fetches = [
            pltpu.make_async_copy(
                intensity_ref.at[slot, :, column * half : (column + 1) * half], measured.at[column], sems.at[column]
            )
            for column in range(2)
        ]
        for fetch in fetches:
            fetch.start()
        twice[:, :size] = probe_ref[...]
        twice[:, size:] = probe_ref[...]
        start[...] = twice[:, pl.ds(shift, size), :]

        @pl.loop(0, kinds)
        def _(kind):
            for place, low in ((0, 0), (1, 1), (2, 0)):
                real = tables_ref[kind, low]
                imag = tables_ref[kind, 2 + low]
                at = size * place
                left[kind, :half, at : at + half] = real
                left[kind, :half, at + half : at + size] = -imag
                left[kind, half:, at : at + half] = imag
                left[kind, half:, at + half : at + size] = real
                right[kind, at : at + half, :half] = real
                right[kind, at : at + half, half:] = imag
                right[kind, at + half : at + size, :half] = -imag
                right[kind, at + half : at + size, half:] = real

        for fetch in fetches:
            fetch.wait()
        source = lax.broadcasted_iota(jnp.int32, (size, size), 0)
        target = lax.broadcasted_iota(jnp.int32, (size, size), 1)
        picked = jnp.where(target < half, 2 * target, 2 * (target - half) + 1)
        sort_rows[...] = (source == picked).astype(jnp.float32).astype(jnp.bfloat16)
        for part in range(2):
            value = jnp.concatenate(
                [measured[column, pl.ds(part, half, stride=2), :] for column in range(2)], axis=1
            )
            total = None
            for _ in range(3):
                high = value.astype(jnp.bfloat16)
                value = value - high.astype(jnp.float32)
                term = jnp.dot(high, sort_rows[...], preferred_element_type=jnp.float32)
                total = term if total is None else total + term
            sorted_ref[part * half : (part + 1) * half] = total

    return pl.pallas_call(
        body,
        out_shape=[
            jax.ShapeDtypeStruct((kinds, size, 3 * size), jnp.bfloat16),
            jax.ShapeDtypeStruct((kinds, 3 * size, size), jnp.bfloat16),
            jax.ShapeDtypeStruct((2, size, size), jnp.float32),
            jax.ShapeDtypeStruct((size, size), jnp.float32),
        ],
        in_specs=[SMEM, VMEM, HBM, VMEM],
        out_specs=[VMEM] * 4,
        scratch_shapes=[
            pltpu.VMEM((2, 2 * size, size), jnp.float32),
            pltpu.VMEM((size, size), jnp.bfloat16),
            pltpu.VMEM((2, size, half), jnp.float32),
            pltpu.SemaphoreType.DMA((2,)),
        ],
        compiler_params=SMALL,
        name="prepare",
    )(control, probe, off_chip(intensity), tables)


def chain(control, owns, halo, left, right, start, measured):
    slices, _, half, size = halo.shape
    low_part = jnp.bfloat16

    def body(*refs):
        control_ref, *own_parts = refs[: slices + 1]
        halo_ref, left_hbm, right_hbm, start_hbm, measured_hbm = refs[slices + 1 : slices + 6]
        grad_parts = refs[slices + 6 : 2 * slices + 6]
        grad_halo, own_ref, grad_own, waves, adjoint, stack, rows, left_ref, right_ref, measured_ref = refs[
            2 * slices + 6 : 2 * slices + 16
        ]
        sems, own_sems, grad_sems = refs[2 * slices + 16 :]
        live = control_ref[0]
        slot = control_ref[1]
        arrivals = [
            pltpu.make_async_copy(
                own_parts[shift], own_ref.at[lax.rem(slot + slices - shift, slices)], own_sems.at[shift]
            )
            for shift in range(slices)
        ]

        def departure(shift):
            return pltpu.make_async_copy(
                grad_own.at[lax.rem(slot + shift, slices)], grad_parts[shift], grad_sems.at[shift]
            )

        near = pl.ds(0, 2)
        rest = pl.ds(2, left_hbm.shape[0] - 2)
        first = [
            pltpu.make_async_copy(start_hbm, waves.at[0], sems.at[0]),
            pltpu.make_async_copy(left_hbm.at[near], left_ref.at[near], sems.at[1]),
            pltpu.make_async_copy(right_hbm.at[near], right_ref.at[near], sems.at[2]),
        ]
        later = [
            pltpu.make_async_copy(left_hbm.at[rest], left_ref.at[rest], sems.at[3]),
            pltpu.make_async_copy(right_hbm.at[rest], right_ref.at[rest], sems.at[4]),
            pltpu.make_async_copy(measured_hbm, measured_ref, sems.at[5]),
        ]

        @pl.when(live == 0)
        def _():
            grad_own[...] = jnp.zeros_like(grad_own)
            grad_halo[...] = jnp.zeros_like(grad_halo)
            for shift in range(slices):
                departure(shift).start()

        def put_stack(branch, part, value):
            high, low = split(value)
            at = part * half
            stack[branch, at : at + half] = high
            stack[branch, size + at : size + at + half] = high
            stack[branch, 2 * size + at : 2 * size + at + half] = low

        def put_rows(branch, block, part, value):
            high, low = split(value)
            at = part * half
            here = slice(block * half, (block + 1) * half)
            rows[branch, here, at : at + half] = high
            rows[branch, here, size + at : size + at + half] = high
            rows[branch, here, 2 * size + at : 2 * size + at + half] = low

        def sandwich(left_kinds, right_kinds, mix):
            for block in range(2):
                middle = jnp.dot(
                    left_ref[left_kinds[block]], stack[block], preferred_element_type=jnp.float32
                )
                for part in range(2):
                    one = middle[part * half : (part + 1) * half, :half]
                    two = middle[part * half : (part + 1) * half, half:]
                    put_rows(0, block, part, one + two if mix else one)
                    put_rows(1, block, part, one - two if mix else two)
            return [
                jnp.dot(rows[branch], right_ref[right_kinds[branch]], preferred_element_type=jnp.float32)
                for branch in range(2)
            ]

        def unmix(first, second, put):
            for column, side in ((0, first + second), (1, first - second)):
                for part in range(2):
                    one = side[:half, part * half : (part + 1) * half]
                    two = side[half:, part * half : (part + 1) * half]
                    put(part, 0, column, one + two)
                    put(part, 1, column, one - two)

        def modulate(index, source, at):
            values = []
            for ref, base in ((own_ref, 0), (halo_ref, half)):
                t_real = 1.0 + ref[index, 0]
                t_imag = ref[index, 1]
                v_real = source[at, 0, base : base + half]
                v_imag = source[at, 1, base : base + half]
                values.append((t_real * v_real - t_imag * v_imag, t_real * v_imag + t_imag * v_real))
            (top_real, top_imag), (low_real, low_imag) = values
            put_stack(0, 0, top_real + low_real)
            put_stack(0, 1, top_imag + low_imag)
            put_stack(1, 0, top_real - low_real)
            put_stack(1, 1, top_imag - low_imag)

        def keep(target, at):
            def put(part, row, column, value):
                target[at, part, row * half : (row + 1) * half, column * half : (column + 1) * half] = value

            return put

        def emit(index):
            for base, target in ((0, grad_own), (half, grad_halo)):
                w_real = waves[index, 0, base : base + half]
                w_imag = waves[index, 1, base : base + half]
                a_real = adjoint[0, 0, base : base + half]
                a_imag = adjoint[0, 1, base : base + half]
                target[index, 0] = w_real * a_real - w_imag * a_imag
                target[index, 1] = -(w_real * a_imag + w_imag * a_real)
            for shift in range(slices):

                @pl.when(lax.rem(slot + shift, slices) == index)
                def _():
                    departure(shift).start()

        @pl.when(live != 0)
        def _():
            for copy in arrivals + first + later:
                copy.start()
            for copy in arrivals + first:
                copy.wait()

            @pl.loop(0, slices - 1)
            def _(index):
                modulate(index, waves, index)
                unmix(*sandwich((0, 1), (0, 1), True), keep(waves, index + 1))

            modulate(slices - 1, waves, slices - 1)
            for copy in later:
                copy.wait()
            for column, far in enumerate(sandwich((2, 3), (2, 4), True)):
                across = slice(column * half, (column + 1) * half)
                for block in range(2):
                    here = slice(block * half, (block + 1) * half)
                    far_real = far[here, :half]
                    far_imag = far[here, half:]
                    misfit = far_real * far_real + far_imag * far_imag - measured_ref[here, across]
                    for part, value in ((0, misfit * far_real), (1, -misfit * far_imag)):
                        high, low = split(value)
                        at = part * half
                        stack[block, at : at + half, across] = high
                        stack[block, size + at : size + at + half, across] = high
                        stack[block, 2 * size + at : 2 * size + at + half, across] = low
            unmix(*sandwich((2, 4), (2, 3), False), keep(adjoint, 0))
            emit(slices - 1)

            @pl.loop(0, slices - 1)
            def _(step):
                index = slices - 1 - step
                modulate(index, adjoint, 0)
                unmix(*sandwich((0, 1), (0, 1), True), keep(adjoint, 0))
                emit(index - 1)

        for shift in range(slices):
            departure(shift).wait()

    return pl.pallas_call(
        body,
        out_shape=[jax.ShapeDtypeStruct(halo.shape[1:], jnp.float32)] * slices + [on_chip(halo.shape)],
        in_specs=[SMEM] + [HBM] * slices + [VMEM] + [HBM] * 4,
        out_specs=[HBM] * slices + [VMEM],
        scratch_shapes=[
            pltpu.VMEM(halo.shape, jnp.float32),
            pltpu.VMEM(halo.shape, jnp.float32),
            pltpu.VMEM((slices, 2, size, size), jnp.float32),
            pltpu.VMEM((1, 2, size, size), jnp.float32),
            pltpu.VMEM((2, 3 * size, size), low_part),
            pltpu.VMEM((2, size, 3 * size), low_part),
            pltpu.VMEM(left.shape, low_part),
            pltpu.VMEM(right.shape, low_part),
            pltpu.VMEM(measured.shape, jnp.float32),
            pltpu.SemaphoreType.DMA((6,)),
            pltpu.SemaphoreType.DMA((slices,)),
            pltpu.SemaphoreType.DMA((slices,)),
        ],
        compiler_params=SMALL,
        name="chain",
    )(
        control,
        *[off_chip(value) for value in owns],
        chip(halo),
        *[off_chip(value) for value in (left, right, start, measured)],
    )


def gather_strip(slot, places, owns, from_above, from_below, width):
    count, planes, strip, size = from_above.shape
    block = 16
    steps = strip // block

    def body(*refs):
        slot_ref, places_ref = refs[:2]
        own_parts = refs[2 : count + 2]
        above_ref, below_ref, out_ref, total, sems = refs[count + 2 :]
        row = lax.broadcasted_iota(jnp.int32, (planes, block, size), 1)

        def copy(step):
            return pltpu.make_async_copy(
                total.at[step % 2], out_ref.at[:, pl.ds(step * block, block)], sems.at[step % 2]
            )

        for step in range(steps):
            here = total.at[step % 2]
            if step >= 2:
                copy(step - 2).wait()
            here[...] = jnp.zeros_like(here)
            across = slice(step * block, (step + 1) * block)
            for group, ref in enumerate((None, above_ref, below_ref)):
                for k in range(count):
                    if group == 0:
                        place = lax.rem(slot_ref[0] + count - k, count)
                        value = own_parts[k][:, across]
                    else:
                        place = k
                        value = ref[k, :, across]
                    start = pl.multiple_of(places_ref[group, place, 1], 128)
                    edge = places_ref[group, place, 0] - step * block
                    if group == 1:
                        value = jnp.where(row < edge, value, 0.0)
                    if group == 2:
                        value = jnp.where(row >= edge, value, 0.0)
                    at = (slice(None), slice(None), pl.ds(start, size))
                    here[at] = here[at] + value
            copy(step).start()
        copy(steps - 2).wait()
        copy(steps - 1).wait()

    return pl.pallas_call(
        body,
        out_shape=jax.ShapeDtypeStruct((planes, strip, width), jnp.float32),
        in_specs=[SMEM, SMEM] + [VMEM] * (count + 2),
        out_specs=HBM,
        scratch_shapes=[
            pltpu.VMEM((2, planes, block, width), jnp.float32),
            pltpu.SemaphoreType.DMA((2,)),
        ],
        compiler_params=SMALL,
        name="gather_strip",
    )(slot, places, *[chip(value) for value in owns], chip(from_above), chip(from_below))


def shifted(values):
    count = len(values)
    return [
        lax.ppermute(value, "cuts", [(i, (i + k) % count) for i in range(count)]) if k else value
        for k, value in enumerate(values)
    ]


def strip_gradient(object_contrast, probe, intensity, positions, counts):
    object_slab = object_contrast[:, 0]
    strip = object_slab.shape[1]
    width = object_slab.shape[2]
    size = probe.shape[-1]
    owner = lax.axis_index("lat")
    slot = lax.axis_index("cuts")
    owners = lax.axis_size("lat")
    downward = [(i, i + 1) for i in range(owners - 1)]
    upward = [(i + 1, i) for i in range(owners - 1)]
    tables = jnp.asarray(wave_tables(size))

    edges = positions[:, 0] - (owner - 1) * strip
    places = jnp.stack([edges, positions[:, 1]], axis=1)
    live = (slot < counts[0]).astype(jnp.int32)
    control = jnp.stack([live, slot, strip - edges[slot]])
    left, right, start, measured = prepare(control, probe, intensity, tables)

    places_above = lax.ppermute(places, "lat", downward)
    places_below = lax.ppermute(places, "lat", upward)
    owns = cut_own(slot[None], object_slab, positions[:, 1], size)
    for_above, for_below = cut_rims(object_slab, places_above, places_below, size)
    from_below = lax.ppermute(for_above, "lat", upward)
    from_above = lax.ppermute(for_below, "lat", downward)
    owns = shifted(owns)
    halo = blend(places, from_above, from_below)
    halo = lax.all_to_all(halo, "cuts", 0, 0, tiled=True)

    *grad_owns, grad_halo = chain(control, owns, halo, left, right, start, measured)

    grad_halo = lax.all_to_all(grad_halo, "cuts", 0, 0, tiled=True)
    back_above = lax.ppermute(grad_halo, "lat", downward)
    back_below = lax.ppermute(grad_halo, "lat", upward)
    grad_owns, grad_halo = lax.optimization_barrier((grad_owns, grad_halo))
    grad_owns = shifted(grad_owns)
    summed = gather_strip(
        slot[None], jnp.stack([places, places_above, places_below]), grad_owns, back_above, back_below, width
    )
    return summed[:, None]


def solution(mesh):
    return jax.shard_map(
        strip_gradient,
        mesh=mesh,
        in_specs=(
            P(None, "cuts", "lat", None),
            P(),
            P("lat", None, None),
            P("lat", None),
            P("lat"),
        ),
        out_specs=P(None, "cuts", "lat", None),
        check_vma=False,
    )
```

```python
import math

import jax
import jax.numpy as jnp
import numpy as np
from jax import lax
from jax.experimental import pallas as pl
from jax.experimental.pallas import tpu as pltpu
from jax.sharding import PartitionSpec as P


PHASE_COEF = 64.0 * math.pi
VMEM = pl.BlockSpec(memory_space=pltpu.VMEM)
SMEM = pl.BlockSpec(memory_space=pltpu.SMEM)
HBM = pl.BlockSpec(memory_space=pltpu.HBM)
ANY = pl.BlockSpec(memory_space=pl.ANY)
SMALL = pltpu.CompilerParams(vmem_limit_bytes=16 * 1024 * 1024)


def on_chip(shape, dtype=jnp.float32):
    return pltpu.VMEM(shape, dtype)


def chip(value):
    return pltpu.with_memory_space_constraint(value, pltpu.VMEM)


def off_chip(value):
    return pltpu.with_memory_space_constraint(value, pltpu.HBM)


def wave_tables(size):
    half = size // 2
    ticks = np.arange(size)
    freqs = np.where(ticks < half, ticks, ticks - size).astype(np.float64)
    turns = (ticks[:, None] * ticks[None, :]) % size
    fourier = np.exp(-2j * np.pi * turns / size) / math.sqrt(size)
    axis_kernel = np.exp(-1j * PHASE_COEF * freqs * freqs / (size * size))
    spread = np.conj(fourier) @ (axis_kernel[:, None] * fourier)
    near = spread[:half, :half]
    across = spread[:half, half:]
    even = fourier[0::2, :half]
    odd = fourier[1::2, :half]
    parts = []
    for table in ((near + across) / 2, (near - across) / 2, even, odd, odd.T):
        for value in (table.real, table.imag):
            high = value.astype(jnp.bfloat16)
            parts += [high, (value - high.astype(np.float64)).astype(jnp.bfloat16)]
    return np.stack(parts).reshape(5, 4, half, half)


def cut_own(slot, object_slab, columns, width):
    count = columns.shape[0]
    planes, rows, _ = object_slab.shape

    def body(slot_ref, columns_ref, slab_ref, *refs):
        sems = refs[count]
        copies = []
        for k in range(count):
            start = pl.multiple_of(columns_ref[lax.rem(slot_ref[0] + k, count)], 128)
            copies.append(
                pltpu.make_async_copy(slab_ref.at[:, :, pl.ds(start, width)], refs[k], sems.at[k])
            )
        for copy in copies:
            copy.start()
        for copy in copies:
            copy.wait()

    return pl.pallas_call(
        body,
        out_shape=[on_chip((planes, rows, width))] * count,
        in_specs=[SMEM, SMEM, HBM],
        out_specs=[VMEM] * count,
        scratch_shapes=[pltpu.SemaphoreType.DMA((count,))],
        compiler_params=SMALL,
        name="cut_own",
    )(slot, columns, off_chip(object_slab))


def cut_rims(object_slab, above, below, width):
    count = above.shape[0]
    planes, rows, _ = object_slab.shape

    def body(above_ref, below_ref, slab_ref, for_above, for_below, sems):
        copies = []
        for side, (places_ref, target) in enumerate(((above_ref, for_above), (below_ref, for_below))):
            for k in range(count):
                start = pl.multiple_of(places_ref[k, 1], 128)
                copies.append(
                    pltpu.make_async_copy(
                        slab_ref.at[:, :, pl.ds(start, width)], target.at[k], sems.at[side, k]
                    )
                )
        for copy in copies:
            copy.start()
        for copy in copies:
            copy.wait()

    return pl.pallas_call(
        body,
        out_shape=[on_chip((count, planes, rows, width))] * 2,
        in_specs=[SMEM, SMEM, HBM],
        out_specs=[VMEM] * 2,
        scratch_shapes=[pltpu.SemaphoreType.DMA((2, count))],
        compiler_params=SMALL,
        name="cut_rims",
    )(above, below, off_chip(object_slab))


def blend(places, from_above, from_below):
    count, planes, rows, width = from_above.shape

    def body(places_ref, above_ref, below_ref, out_ref):
        row = lax.broadcasted_iota(jnp.int32, (planes, rows, width), 1)
        for k in range(count):
            out_ref[k] = jnp.where(row < places_ref[k, 0], below_ref[k], above_ref[k])

    return pl.pallas_call(
        body,
        out_shape=on_chip(from_above.shape),
        in_specs=[SMEM, VMEM, VMEM],
        out_specs=VMEM,
        compiler_params=SMALL,
        name="blend",
    )(places, chip(from_above), chip(from_below))


def split(value):
    high = value.astype(jnp.bfloat16)
    return high, (value - high.astype(jnp.float32)).astype(jnp.bfloat16)


def prepare(control, probe, intensity, tables):
    size = probe.shape[-1]
    half = size // 2
    kinds = tables.shape[0]

    def body(control_ref, probe_ref, intensity_ref, tables_ref, left, right, start, sorted_ref, twice, sort_rows, measured, sems):
        slot = control_ref[1]
        shift = pl.multiple_of(control_ref[2], 8)
        fetches = [
            pltpu.make_async_copy(
                intensity_ref.at[slot, :, column * half : (column + 1) * half], measured.at[column], sems.at[column]
            )
            for column in range(2)
        ]
        for fetch in fetches:
            fetch.start()
        twice[:, :size] = probe_ref[...]
        twice[:, size:] = probe_ref[...]
        start[...] = twice[:, pl.ds(shift, size), :]

        @pl.loop(0, kinds)
        def _(kind):
            for place, low in ((0, 0), (1, 1), (2, 0)):
                real = tables_ref[kind, low]
                imag = tables_ref[kind, 2 + low]
                at = size * place
                left[kind, :half, at : at + half] = real
                left[kind, :half, at + half : at + size] = -imag
                left[kind, half:, at : at + half] = imag
                left[kind, half:, at + half : at + size] = real
                right[kind, at : at + half, :half] = real
                right[kind, at : at + half, half:] = imag
                right[kind, at + half : at + size, :half] = -imag
                right[kind, at + half : at + size, half:] = real

        for fetch in fetches:
            fetch.wait()
        source = lax.broadcasted_iota(jnp.int32, (size, size), 0)
        target = lax.broadcasted_iota(jnp.int32, (size, size), 1)
        picked = jnp.where(target < half, 2 * target, 2 * (target - half) + 1)
        sort_rows[...] = (source == picked).astype(jnp.float32).astype(jnp.bfloat16)
        for part in range(2):
            value = jnp.concatenate(
                [measured[column, pl.ds(part, half, stride=2), :] for column in range(2)], axis=1
            )
            total = None
            for _ in range(3):
                high = value.astype(jnp.bfloat16)
                value = value - high.astype(jnp.float32)
                term = jnp.dot(high, sort_rows[...], preferred_element_type=jnp.float32)
                total = term if total is None else total + term
            sorted_ref[part * half : (part + 1) * half] = total

    return pl.pallas_call(
        body,
        out_shape=[
            pltpu.HBM((kinds, size, 3 * size), jnp.bfloat16),
            pltpu.HBM((kinds, 3 * size, size), jnp.bfloat16),
            pltpu.HBM((2, size, size), jnp.float32),
            pltpu.HBM((size, size), jnp.float32),
        ],
        in_specs=[SMEM, VMEM, HBM, VMEM],
        out_specs=[VMEM] * 4,
        scratch_shapes=[
            pltpu.VMEM((2, 2 * size, size), jnp.float32),
            pltpu.VMEM((size, size), jnp.bfloat16),
            pltpu.VMEM((2, size, half), jnp.float32),
            pltpu.SemaphoreType.DMA((2,)),
        ],
        compiler_params=SMALL,
        name="prepare",
    )(control, probe, off_chip(intensity), tables)


def chain(control, owns, halo, left, right, start, measured):
    slices, _, half, size = halo.shape
    low_part = jnp.bfloat16

    def body(*refs):
        control_ref, *own_parts = refs[: slices + 1]
        halo_ref, left_hbm, right_hbm, start_hbm, measured_hbm = refs[slices + 1 : slices + 6]
        grad_parts = refs[slices + 6 : 2 * slices + 6]
        grad_halo, own_ref, grad_own, waves, adjoint, stack, rows, left_ref, right_ref, measured_ref = refs[
            2 * slices + 6 : 2 * slices + 16
        ]
        sems, own_sems, grad_sems = refs[2 * slices + 16 :]
        live = control_ref[0]
        slot = control_ref[1]
        arrivals = [
            pltpu.make_async_copy(
                own_parts[shift], own_ref.at[lax.rem(slot + slices - shift, slices)], own_sems.at[shift]
            )
            for shift in range(slices)
        ]

        def departure(shift):
            return pltpu.make_async_copy(
                grad_own.at[lax.rem(slot + shift, slices)], grad_parts[shift], grad_sems.at[shift]
            )

        near = pl.ds(0, 2)
        rest = pl.ds(2, left_hbm.shape[0] - 2)
        first = [
            pltpu.make_async_copy(start_hbm, waves.at[0], sems.at[0]),
            pltpu.make_async_copy(left_hbm.at[near], left_ref.at[near], sems.at[1]),
            pltpu.make_async_copy(right_hbm.at[near], right_ref.at[near], sems.at[2]),
        ]
        later = [
            pltpu.make_async_copy(left_hbm.at[rest], left_ref.at[rest], sems.at[3]),
            pltpu.make_async_copy(right_hbm.at[rest], right_ref.at[rest], sems.at[4]),
            pltpu.make_async_copy(measured_hbm, measured_ref, sems.at[5]),
        ]

        @pl.when(live == 0)
        def _():
            grad_own[...] = jnp.zeros_like(grad_own)
            grad_halo[...] = jnp.zeros_like(grad_halo)
            for shift in range(slices):
                departure(shift).start()

        def put_stack(branch, part, value):
            high, low = split(value)
            at = part * half
            stack[branch, at : at + half] = high
            stack[branch, size + at : size + at + half] = high
            stack[branch, 2 * size + at : 2 * size + at + half] = low

        def put_rows(branch, block, part, value):
            high, low = split(value)
            at = part * half
            here = slice(block * half, (block + 1) * half)
            rows[branch, here, at : at + half] = high
            rows[branch, here, size + at : size + at + half] = high
            rows[branch, here, 2 * size + at : 2 * size + at + half] = low

        def sandwich(left_kinds, right_kinds, mix):
            for block in range(2):
                middle = jnp.dot(
                    left_ref[left_kinds[block]], stack[block], preferred_element_type=jnp.float32
                )
                for part in range(2):
                    one = middle[part * half : (part + 1) * half, :half]
                    two = middle[part * half : (part + 1) * half, half:]
                    put_rows(0, block, part, one + two if mix else one)
                    put_rows(1, block, part, one - two if mix else two)
            return [
                jnp.dot(rows[branch], right_ref[right_kinds[branch]], preferred_element_type=jnp.float32)
                for branch in range(2)
            ]

        def unmix(first, second, put):
            for column, side in ((0, first + second), (1, first - second)):
                for part in range(2):
                    one = side[:half, part * half : (part + 1) * half]
                    two = side[half:, part * half : (part + 1) * half]
                    put(part, 0, column, one + two)
                    put(part, 1, column, one - two)

        def modulate(index, source, at):
            values = []
            for ref, base in ((own_ref, 0), (halo_ref, half)):
                t_real = 1.0 + ref[index, 0]
                t_imag = ref[index, 1]
                v_real = source[at, 0, base : base + half]
                v_imag = source[at, 1, base : base + half]
                values.append((t_real * v_real - t_imag * v_imag, t_real * v_imag + t_imag * v_real))
            (top_real, top_imag), (low_real, low_imag) = values
            put_stack(0, 0, top_real + low_real)
            put_stack(0, 1, top_imag + low_imag)
            put_stack(1, 0, top_real - low_real)
            put_stack(1, 1, top_imag - low_imag)

        def keep(target, at):
            def put(part, row, column, value):
                target[at, part, row * half : (row + 1) * half, column * half : (column + 1) * half] = value

            return put

        def emit(index):
            for base, target in ((0, grad_own), (half, grad_halo)):
                w_real = waves[index, 0, base : base + half]
                w_imag = waves[index, 1, base : base + half]
                a_real = adjoint[0, 0, base : base + half]
                a_imag = adjoint[0, 1, base : base + half]
                target[index, 0] = w_real * a_real - w_imag * a_imag
                target[index, 1] = -(w_real * a_imag + w_imag * a_real)
            for shift in range(slices):

                @pl.when(lax.rem(slot + shift, slices) == index)
                def _():
                    departure(shift).start()

        @pl.when(live != 0)
        def _():
            for copy in arrivals + first + later:
                copy.start()
            for copy in arrivals + first:
                copy.wait()

            @pl.loop(0, slices - 1)
            def _(index):
                modulate(index, waves, index)
                unmix(*sandwich((0, 1), (0, 1), True), keep(waves, index + 1))

            modulate(slices - 1, waves, slices - 1)
            for copy in later:
                copy.wait()
            for column, far in enumerate(sandwich((2, 3), (2, 4), True)):
                across = slice(column * half, (column + 1) * half)
                for block in range(2):
                    here = slice(block * half, (block + 1) * half)
                    far_real = far[here, :half]
                    far_imag = far[here, half:]
                    misfit = far_real * far_real + far_imag * far_imag - measured_ref[here, across]
                    for part, value in ((0, misfit * far_real), (1, -misfit * far_imag)):
                        high, low = split(value)
                        at = part * half
                        stack[block, at : at + half, across] = high
                        stack[block, size + at : size + at + half, across] = high
                        stack[block, 2 * size + at : 2 * size + at + half, across] = low
            unmix(*sandwich((2, 4), (2, 3), False), keep(adjoint, 0))
            emit(slices - 1)

            @pl.loop(0, slices - 1)
            def _(step):
                index = slices - 1 - step
                modulate(index, adjoint, 0)
                unmix(*sandwich((0, 1), (0, 1), True), keep(adjoint, 0))
                emit(index - 1)

        for shift in range(slices):
            departure(shift).wait()

    return pl.pallas_call(
        body,
        out_shape=[jax.ShapeDtypeStruct(halo.shape[1:], jnp.float32)] * slices + [on_chip(halo.shape)],
        in_specs=[SMEM] + [ANY] * slices + [VMEM] + [HBM] * 4,
        out_specs=[HBM] * slices + [VMEM],
        scratch_shapes=[
            pltpu.VMEM(halo.shape, jnp.float32),
            pltpu.VMEM(halo.shape, jnp.float32),
            pltpu.VMEM((slices, 2, size, size), jnp.float32),
            pltpu.VMEM((1, 2, size, size), jnp.float32),
            pltpu.VMEM((2, 3 * size, size), low_part),
            pltpu.VMEM((2, size, 3 * size), low_part),
            pltpu.VMEM(left.shape, low_part),
            pltpu.VMEM(right.shape, low_part),
            pltpu.VMEM(measured.shape, jnp.float32),
            pltpu.SemaphoreType.DMA((6,)),
            pltpu.SemaphoreType.DMA((slices,)),
            pltpu.SemaphoreType.DMA((slices,)),
        ],
        compiler_params=SMALL,
        name="chain",
    )(
        control,
        *owns,
        chip(halo),
        *[off_chip(value) for value in (left, right, start, measured)],
    )


def gather_rims(above, below, from_above, from_below, width):
    count, planes, strip, size = from_above.shape

    def body(places_above, places_below, above_ref, below_ref, out_ref):
        row = lax.broadcasted_iota(jnp.int32, (planes, strip, size), 1)
        out_ref[...] = jnp.zeros_like(out_ref)
        for places_ref, ref, upper in ((places_above, above_ref, True), (places_below, below_ref, False)):
            for k in range(count):
                start = pl.multiple_of(places_ref[k, 1], 128)
                mask = row < places_ref[k, 0] if upper else row >= places_ref[k, 0]
                at = (slice(None), slice(None), pl.ds(start, size))
                out_ref[at] = out_ref[at] + jnp.where(mask, ref[k], 0.0)

    return pl.pallas_call(
        body,
        out_shape=on_chip((planes, strip, width)),
        in_specs=[SMEM, SMEM, VMEM, VMEM],
        out_specs=VMEM,
        compiler_params=SMALL,
        name="gather_rims",
    )(above, below, chip(from_above), chip(from_below))


def gather_strip(slot, places, owns, rims):
    count = len(owns)
    _, strip, size = owns[0].shape
    block = 32
    steps = strip // block

    def body(slot_ref, places_ref, rims_ref, *refs):
        out_ref, total, sems = refs[count:]

        def copy(step):
            here = pl.ds(step * block, block)
            return pltpu.make_async_copy(total.at[:, here], out_ref.at[:, here], sems.at[step])

        for step in range(steps):
            across = slice(step * block, (step + 1) * block)
            total[:, across] = rims_ref[:, across]
            for k in range(count):
                start = pl.multiple_of(places_ref[lax.rem(slot_ref[0] + count - k, count), 1], 128)
                at = (slice(None), across, pl.ds(start, size))
                total[at] = total[at] + refs[k][:, across]
            copy(step).start()
        for step in range(steps):
            copy(step).wait()

    return pl.pallas_call(
        body,
        out_shape=jax.ShapeDtypeStruct(rims.shape, jnp.float32),
        in_specs=[SMEM, SMEM] + [VMEM] * (count + 1),
        out_specs=HBM,
        scratch_shapes=[
            pltpu.VMEM(rims.shape, jnp.float32),
            pltpu.SemaphoreType.DMA((steps,)),
        ],
        compiler_params=SMALL,
        name="gather_strip",
    )(slot, places, chip(rims), *[chip(value) for value in owns])


def steering(slot, counts, places, strip):
    def body(slot_ref, counts_ref, places_ref, out_ref):
        slot = slot_ref[0]
        out_ref[0] = (slot < counts_ref[0]).astype(jnp.int32)
        out_ref[1] = slot
        out_ref[2] = strip - places_ref[slot, 0]

    return pl.pallas_call(
        body,
        out_shape=jax.ShapeDtypeStruct((3,), jnp.int32),
        in_specs=[SMEM] * 3,
        out_specs=SMEM,
        compiler_params=SMALL,
        name="steering",
    )(slot, counts, places)


def shifted(values):
    count = len(values)
    return [
        lax.ppermute(value, "cuts", [(i, (i + k) % count) for i in range(count)]) if k else value
        for k, value in enumerate(values)
    ]


def strip_gradient(object_contrast, probe, intensity, positions, counts):
    object_slab = object_contrast[:, 0]
    strip = object_slab.shape[1]
    width = object_slab.shape[2]
    size = probe.shape[-1]
    owner = lax.axis_index("lat")
    slot = lax.axis_index("cuts")
    owners = lax.axis_size("lat")
    downward = [(i, i + 1) for i in range(owners - 1)]
    upward = [(i + 1, i) for i in range(owners - 1)]
    tables = jnp.asarray(wave_tables(size))

    edges = positions[:, 0] - (owner - 1) * strip
    places = jnp.stack([edges, positions[:, 1]], axis=1)
    slot = slot[None]
    places_above = lax.ppermute(places, "lat", downward)
    places_below = lax.ppermute(places, "lat", upward)
    owns = cut_own(slot, object_slab, positions[:, 1], size)
    for_above, for_below = cut_rims(object_slab, places_above, places_below, size)
    from_below = lax.ppermute(for_above, "lat", upward)
    from_above = lax.ppermute(for_below, "lat", downward)
    owns = shifted(owns)
    control = steering(slot, counts, places, strip)
    left, right, start, measured = prepare(control, probe, intensity, tables)
    halo = blend(places, from_above, from_below)
    halo = lax.all_to_all(halo, "cuts", 0, 0, tiled=True)

    *grad_owns, grad_halo = chain(control, owns, halo, left, right, start, measured)

    grad_halo = lax.all_to_all(grad_halo, "cuts", 0, 0, tiled=True)
    back_above = lax.ppermute(grad_halo, "lat", downward)
    back_below = lax.ppermute(grad_halo, "lat", upward)
    grad_owns, grad_halo = lax.optimization_barrier((grad_owns, grad_halo))
    grad_owns = shifted(grad_owns)
    rims = gather_rims(places_above, places_below, back_above, back_below, width)
    summed = gather_strip(slot, places, grad_owns, rims)
    return summed[:, None]


def solution(mesh):
    return jax.shard_map(
        strip_gradient,
        mesh=mesh,
        in_specs=(
            P(None, "cuts", "lat", None),
            P(),
            P("lat", None, None),
            P("lat", None),
            P("lat"),
        ),
        out_specs=P(None, "cuts", "lat", None),
        check_vma=False,
    )
```

```python
import math

import jax
import jax.numpy as jnp
import numpy as np
from jax import lax
from jax.experimental import pallas as pl
from jax.experimental.pallas import tpu as pltpu
from jax.sharding import PartitionSpec as P


PHASE_COEF = 64.0 * math.pi
VMEM = pl.BlockSpec(memory_space=pltpu.VMEM)
SMEM = pl.BlockSpec(memory_space=pltpu.SMEM)
HBM = pl.BlockSpec(memory_space=pltpu.HBM)
ANY = pl.BlockSpec(memory_space=pl.ANY)
SMALL = pltpu.CompilerParams(vmem_limit_bytes=16 * 1024 * 1024)


def on_chip(shape, dtype=jnp.float32):
    return pltpu.VMEM(shape, dtype)


def chip(value):
    return pltpu.with_memory_space_constraint(value, pltpu.VMEM)


def off_chip(value):
    return pltpu.with_memory_space_constraint(value, pltpu.HBM)


def wave_tables(size):
    half = size // 2
    ticks = np.arange(size)
    freqs = np.where(ticks < half, ticks, ticks - size).astype(np.float64)
    turns = (ticks[:, None] * ticks[None, :]) % size
    fourier = np.exp(-2j * np.pi * turns / size) / math.sqrt(size)
    axis_kernel = np.exp(-1j * PHASE_COEF * freqs * freqs / (size * size))
    spread = np.conj(fourier) @ (axis_kernel[:, None] * fourier)
    near = spread[:half, :half]
    across = spread[:half, half:]
    even = fourier[0::2, :half]
    odd = fourier[1::2, :half]
    parts = []
    for table in ((near + across) / 2, (near - across) / 2, even, odd, odd.T):
        for value in (table.real, table.imag):
            high = value.astype(jnp.bfloat16)
            parts += [high, (value - high.astype(np.float64)).astype(jnp.bfloat16)]
    return np.stack(parts).reshape(5, 4, half, half)


def cut_own(here, object_slab, positions, width):
    count = positions.shape[0]
    planes, rows, _ = object_slab.shape

    def body(here_ref, positions_ref, slab_ref, *refs):
        sems = refs[count]
        copies = []
        for k in range(count):
            start = pl.multiple_of(positions_ref[lax.rem(here_ref[0] + k, count), 1], 128)
            copies.append(
                pltpu.make_async_copy(slab_ref.at[:, :, pl.ds(start, width)], refs[k], sems.at[k])
            )
        for copy in copies:
            copy.start()
        for copy in copies:
            copy.wait()

    return pl.pallas_call(
        body,
        out_shape=[on_chip((planes, rows, width))] * count,
        in_specs=[SMEM, SMEM, HBM],
        out_specs=[VMEM] * count,
        scratch_shapes=[pltpu.SemaphoreType.DMA((count,))],
        compiler_params=SMALL,
        name="cut_own",
    )(here, positions, off_chip(object_slab))


def cut_rims(object_slab, outer, inner, width):
    count = outer.shape[0]
    planes, rows, _ = object_slab.shape

    def body(outer_ref, inner_ref, slab_ref, for_outer, for_inner, sems):
        copies = []
        for side, (positions_ref, target) in enumerate(((outer_ref, for_outer), (inner_ref, for_inner))):
            for k in range(count):
                start = pl.multiple_of(positions_ref[k, 1], 128)
                copies.append(
                    pltpu.make_async_copy(
                        slab_ref.at[:, :, pl.ds(start, width)], target.at[k], sems.at[side, k]
                    )
                )
        for copy in copies:
            copy.start()
        for copy in copies:
            copy.wait()

    return pl.pallas_call(
        body,
        out_shape=[on_chip((count, planes, rows, width))] * 2,
        in_specs=[SMEM, SMEM, HBM],
        out_specs=[VMEM] * 2,
        scratch_shapes=[pltpu.SemaphoreType.DMA((2, count))],
        compiler_params=SMALL,
        name="cut_rims",
    )(outer, inner, off_chip(object_slab))


def blend(here, positions, from_outer, from_inner):
    count, planes, rows, width = from_outer.shape

    def body(here_ref, positions_ref, outer_ref, inner_ref, *out_refs):
        row = lax.broadcasted_iota(jnp.int32, (planes, rows, width), 1)
        owner = here_ref[1]
        for shift in range(count):
            k = lax.rem(here_ref[0] + shift, count)
            edge = positions_ref[k, 0] - (owner - 1) * rows

            @pl.when(lax.rem(owner, 2) == 1)
            def _():
                out_refs[shift][...] = jnp.where(row < edge, outer_ref[k], inner_ref[k])

            @pl.when(lax.rem(owner, 2) == 0)
            def _():
                out_refs[shift][...] = jnp.where(row < edge, inner_ref[k], outer_ref[k])

    return pl.pallas_call(
        body,
        out_shape=[on_chip((planes, rows, width))] * count,
        in_specs=[SMEM, SMEM, VMEM, VMEM],
        out_specs=[VMEM] * count,
        compiler_params=SMALL,
        name="blend",
    )(here, positions, chip(from_outer), chip(from_inner))


def split(value):
    high = value.astype(jnp.bfloat16)
    return high, (value - high.astype(jnp.float32)).astype(jnp.bfloat16)


def prepare(control, probe, intensity, tables):
    size = probe.shape[-1]
    half = size // 2
    kinds = tables.shape[0]

    def body(control_ref, probe_ref, intensity_ref, tables_ref, left, right, start, sorted_ref, twice, sort_rows, measured, sems):
        slot = control_ref[1]
        shift = pl.multiple_of(control_ref[2], 8)
        fetches = [
            pltpu.make_async_copy(
                intensity_ref.at[slot, :, column * half : (column + 1) * half], measured.at[column], sems.at[column]
            )
            for column in range(2)
        ]
        for fetch in fetches:
            fetch.start()
        twice[:, :size] = probe_ref[...]
        twice[:, size:] = probe_ref[...]
        start[...] = twice[:, pl.ds(shift, size), :]

        @pl.loop(0, kinds)
        def _(kind):
            for place, low in ((0, 0), (1, 1), (2, 0)):
                real = tables_ref[kind, low]
                imag = tables_ref[kind, 2 + low]
                at = size * place
                left[kind, :half, at : at + half] = real
                left[kind, :half, at + half : at + size] = -imag
                left[kind, half:, at : at + half] = imag
                left[kind, half:, at + half : at + size] = real
                right[kind, at : at + half, :half] = real
                right[kind, at : at + half, half:] = imag
                right[kind, at + half : at + size, :half] = -imag
                right[kind, at + half : at + size, half:] = real

        for fetch in fetches:
            fetch.wait()
        source = lax.broadcasted_iota(jnp.int32, (size, size), 0)
        target = lax.broadcasted_iota(jnp.int32, (size, size), 1)
        picked = jnp.where(target < half, 2 * target, 2 * (target - half) + 1)
        sort_rows[...] = (source == picked).astype(jnp.float32).astype(jnp.bfloat16)
        for part in range(2):
            value = jnp.concatenate(
                [measured[column, pl.ds(part, half, stride=2), :] for column in range(2)], axis=1
            )
            total = None
            for _ in range(3):
                high = value.astype(jnp.bfloat16)
                value = value - high.astype(jnp.float32)
                term = jnp.dot(high, sort_rows[...], preferred_element_type=jnp.float32)
                total = term if total is None else total + term
            sorted_ref[part * half : (part + 1) * half] = total

    return pl.pallas_call(
        body,
        out_shape=[
            pltpu.HBM((kinds, size, 3 * size), jnp.bfloat16),
            pltpu.HBM((kinds, 3 * size, size), jnp.bfloat16),
            pltpu.HBM((2, size, size), jnp.float32),
            pltpu.HBM((size, size), jnp.float32),
        ],
        in_specs=[SMEM, VMEM, HBM, VMEM],
        out_specs=[VMEM] * 4,
        scratch_shapes=[
            pltpu.VMEM((2, 2 * size, size), jnp.float32),
            pltpu.VMEM((size, size), jnp.bfloat16),
            pltpu.VMEM((2, size, half), jnp.float32),
            pltpu.SemaphoreType.DMA((2,)),
        ],
        compiler_params=SMALL,
        name="prepare",
    )(control, probe, off_chip(intensity), tables)


def chain(control, owns, halos, left, right, start, measured):
    slices = len(owns)
    _, half, size = owns[0].shape
    shape = (slices, 2, half, size)
    low_part = jnp.bfloat16

    def body(*refs):
        control_ref, *parts = refs[: 2 * slices + 1]
        refs = refs[2 * slices + 1 :]
        left_hbm, right_hbm, start_hbm, measured_hbm = refs[:4]
        grad_parts = refs[4 : slices + 4]
        grad_halo, own_ref, halo_ref, grad_own, waves, adjoint, stack, rows, left_ref, right_ref, measured_ref = refs[
            slices + 4 : slices + 15
        ]
        sems, own_sems, halo_sems, grad_sems = refs[slices + 15 :]
        live = control_ref[0]
        slot = control_ref[1]

        def arrivals(shift, index):
            return (
                pltpu.make_async_copy(parts[shift], own_ref.at[index], own_sems.at[index]),
                pltpu.make_async_copy(parts[slices + shift], halo_ref.at[index], halo_sems.at[index]),
            )

        def arrive(index):
            for copy in arrivals(0, index):
                copy.wait()

        def departure(shift):
            return pltpu.make_async_copy(
                grad_own.at[lax.rem(slot + shift, slices)], grad_parts[shift], grad_sems.at[shift]
            )

        near = pl.ds(0, 2)
        rest = pl.ds(2, left_hbm.shape[0] - 2)
        first = [
            pltpu.make_async_copy(start_hbm, waves.at[0], sems.at[0]),
            pltpu.make_async_copy(left_hbm.at[near], left_ref.at[near], sems.at[1]),
            pltpu.make_async_copy(right_hbm.at[near], right_ref.at[near], sems.at[2]),
        ]
        later = [
            pltpu.make_async_copy(left_hbm.at[rest], left_ref.at[rest], sems.at[3]),
            pltpu.make_async_copy(right_hbm.at[rest], right_ref.at[rest], sems.at[4]),
            pltpu.make_async_copy(measured_hbm, measured_ref, sems.at[5]),
        ]

        @pl.when(live == 0)
        def _():
            grad_own[...] = jnp.zeros_like(grad_own)
            grad_halo[...] = jnp.zeros_like(grad_halo)
            for shift in range(slices):
                departure(shift).start()

        def put_stack(branch, part, value):
            high, low = split(value)
            at = part * half
            stack[branch, at : at + half] = high
            stack[branch, size + at : size + at + half] = high
            stack[branch, 2 * size + at : 2 * size + at + half] = low

        def put_rows(branch, block, part, value):
            high, low = split(value)
            at = part * half
            here = slice(block * half, (block + 1) * half)
            rows[branch, here, at : at + half] = high
            rows[branch, here, size + at : size + at + half] = high
            rows[branch, here, 2 * size + at : 2 * size + at + half] = low

        def sandwich(left_kinds, right_kinds, mix):
            for block in range(2):
                middle = jnp.dot(
                    left_ref[left_kinds[block]], stack[block], preferred_element_type=jnp.float32
                )
                for part in range(2):
                    one = middle[part * half : (part + 1) * half, :half]
                    two = middle[part * half : (part + 1) * half, half:]
                    put_rows(0, block, part, one + two if mix else one)
                    put_rows(1, block, part, one - two if mix else two)
            return [
                jnp.dot(rows[branch], right_ref[right_kinds[branch]], preferred_element_type=jnp.float32)
                for branch in range(2)
            ]

        def unmix(first, second, put):
            for column, side in ((0, first + second), (1, first - second)):
                for part in range(2):
                    one = side[:half, part * half : (part + 1) * half]
                    two = side[half:, part * half : (part + 1) * half]
                    put(part, 0, column, one + two)
                    put(part, 1, column, one - two)

        def modulate(index, source, at):
            values = []
            for ref, base in ((own_ref, 0), (halo_ref, half)):
                t_real = 1.0 + ref[index, 0]
                t_imag = ref[index, 1]
                v_real = source[at, 0, base : base + half]
                v_imag = source[at, 1, base : base + half]
                values.append((t_real * v_real - t_imag * v_imag, t_real * v_imag + t_imag * v_real))
            (top_real, top_imag), (low_real, low_imag) = values
            put_stack(0, 0, top_real + low_real)
            put_stack(0, 1, top_imag + low_imag)
            put_stack(1, 0, top_real - low_real)
            put_stack(1, 1, top_imag - low_imag)

        def keep(target, at):
            def put(part, row, column, value):
                target[at, part, row * half : (row + 1) * half, column * half : (column + 1) * half] = value

            return put

        def emit(index):
            for base, target in ((0, grad_own), (half, grad_halo)):
                w_real = waves[index, 0, base : base + half]
                w_imag = waves[index, 1, base : base + half]
                a_real = adjoint[0, 0, base : base + half]
                a_imag = adjoint[0, 1, base : base + half]
                target[index, 0] = w_real * a_real - w_imag * a_imag
                target[index, 1] = -(w_real * a_imag + w_imag * a_real)
            for shift in range(slices):

                @pl.when(lax.rem(slot + shift, slices) == index)
                def _():
                    departure(shift).start()

        @pl.when(live != 0)
        def _():
            for shift in range(slices):
                for copy in arrivals(shift, lax.rem(slot + slices - shift, slices)):
                    copy.start()
            for copy in first + later:
                copy.start()
            for copy in first:
                copy.wait()

            @pl.loop(0, slices - 1)
            def _(index):
                arrive(index)
                modulate(index, waves, index)
                unmix(*sandwich((0, 1), (0, 1), True), keep(waves, index + 1))

            arrive(slices - 1)
            modulate(slices - 1, waves, slices - 1)
            for copy in later:
                copy.wait()
            for column, far in enumerate(sandwich((2, 3), (2, 4), True)):
                across = slice(column * half, (column + 1) * half)
                for block in range(2):
                    here = slice(block * half, (block + 1) * half)
                    far_real = far[here, :half]
                    far_imag = far[here, half:]
                    misfit = far_real * far_real + far_imag * far_imag - measured_ref[here, across]
                    for part, value in ((0, misfit * far_real), (1, -misfit * far_imag)):
                        high, low = split(value)
                        at = part * half
                        stack[block, at : at + half, across] = high
                        stack[block, size + at : size + at + half, across] = high
                        stack[block, 2 * size + at : 2 * size + at + half, across] = low
            unmix(*sandwich((2, 4), (2, 3), False), keep(adjoint, 0))
            emit(slices - 1)

            @pl.loop(0, slices - 1)
            def _(step):
                index = slices - 1 - step
                modulate(index, adjoint, 0)
                unmix(*sandwich((0, 1), (0, 1), True), keep(adjoint, 0))
                emit(index - 1)

        for shift in range(slices):
            departure(shift).wait()

    return pl.pallas_call(
        body,
        out_shape=[jax.ShapeDtypeStruct(shape[1:], jnp.float32)] * slices + [on_chip(shape)],
        in_specs=[SMEM] + [ANY] * (2 * slices) + [HBM] * 4,
        out_specs=[HBM] * slices + [VMEM],
        scratch_shapes=[
            pltpu.VMEM(shape, jnp.float32),
            pltpu.VMEM(shape, jnp.float32),
            pltpu.VMEM(shape, jnp.float32),
            pltpu.VMEM((slices, 2, size, size), jnp.float32),
            pltpu.VMEM((1, 2, size, size), jnp.float32),
            pltpu.VMEM((2, 3 * size, size), low_part),
            pltpu.VMEM((2, size, 3 * size), low_part),
            pltpu.VMEM(left.shape, low_part),
            pltpu.VMEM(right.shape, low_part),
            pltpu.VMEM(measured.shape, jnp.float32),
            pltpu.SemaphoreType.DMA((6,)),
            pltpu.SemaphoreType.DMA((slices,)),
            pltpu.SemaphoreType.DMA((slices,)),
            pltpu.SemaphoreType.DMA((slices,)),
        ],
        compiler_params=SMALL,
        name="chain",
    )(
        control,
        *owns,
        *halos,
        *[off_chip(value) for value in (left, right, start, measured)],
    )


def gather_rims(here, outer, inner, from_outer, from_inner, width):
    count, planes, strip, size = from_outer.shape

    def body(here_ref, outer_places, inner_places, outer_ref, inner_ref, out_ref):
        owner = here_ref[1]
        row = lax.broadcasted_iota(jnp.int32, (planes, strip, size), 1)
        out_ref[...] = jnp.zeros_like(out_ref)

        def add(places_ref, ref, upper):
            for k in range(count):
                start = pl.multiple_of(places_ref[k, 1], 128)
                if upper:
                    mask = row < places_ref[k, 0] - (owner - 2) * strip
                else:
                    mask = row >= places_ref[k, 0] - owner * strip
                at = (slice(None), slice(None), pl.ds(start, size))
                out_ref[at] = out_ref[at] + jnp.where(mask, ref[k], 0.0)

        @pl.when(lax.rem(owner, 2) == 1)
        def _():
            add(inner_places, inner_ref, True)
            add(outer_places, outer_ref, False)

        @pl.when(lax.rem(owner, 2) == 0)
        def _():
            add(outer_places, outer_ref, True)
            add(inner_places, inner_ref, False)

    return pl.pallas_call(
        body,
        out_shape=on_chip((planes, strip, width)),
        in_specs=[SMEM] * 3 + [VMEM] * 2,
        out_specs=VMEM,
        compiler_params=SMALL,
        name="gather_rims",
    )(here, outer, inner, chip(from_outer), chip(from_inner))


def gather_strip(slot, places, owns, rims):
    count = len(owns)
    _, strip, size = owns[0].shape
    block = 32
    steps = strip // block

    def body(slot_ref, places_ref, rims_ref, *refs):
        out_ref, total, sems = refs[count:]

        def copy(step):
            here = pl.ds(step * block, block)
            return pltpu.make_async_copy(total.at[:, here], out_ref.at[:, here], sems.at[step])

        for step in range(steps):
            across = slice(step * block, (step + 1) * block)
            total[:, across] = rims_ref[:, across]
            for k in range(count):
                start = pl.multiple_of(places_ref[lax.rem(slot_ref[0] + count - k, count), 1], 128)
                at = (slice(None), across, pl.ds(start, size))
                total[at] = total[at] + refs[k][:, across]
            copy(step).start()
        for step in range(steps):
            copy(step).wait()

    return pl.pallas_call(
        body,
        out_shape=jax.ShapeDtypeStruct(rims.shape, jnp.float32),
        in_specs=[SMEM, SMEM] + [VMEM] * (count + 1),
        out_specs=HBM,
        scratch_shapes=[
            pltpu.VMEM(rims.shape, jnp.float32),
            pltpu.SemaphoreType.DMA((steps,)),
        ],
        compiler_params=SMALL,
        name="gather_strip",
    )(slot, places, chip(rims), *[chip(value) for value in owns])


def steering(here, counts, positions, strip):
    def body(here_ref, counts_ref, positions_ref, out_ref):
        slot = here_ref[0]
        out_ref[0] = (slot < counts_ref[0]).astype(jnp.int32)
        out_ref[1] = slot
        out_ref[2] = here_ref[1] * strip - positions_ref[slot, 0]

    return pl.pallas_call(
        body,
        out_shape=jax.ShapeDtypeStruct((3,), jnp.int32),
        in_specs=[SMEM] * 3,
        out_specs=SMEM,
        compiler_params=SMALL,
        name="steering",
    )(here, counts, positions)


def shifted(values):
    count = len(values)
    return [
        lax.ppermute(value, "cuts", [(i, (i + k) % count) for i in range(count)]) if k else value
        for k, value in enumerate(values)
    ]


def strip_gradient(object_contrast, probe, intensity, positions, counts):
    object_slab = object_contrast[:, 0]
    strip = object_slab.shape[1]
    width = object_slab.shape[2]
    size = probe.shape[-1]
    owners = lax.axis_size("lat")
    here = jnp.stack([lax.axis_index("cuts"), lax.axis_index("lat")])
    outer = [(i, i + 1) for i in range(1, owners - 1, 2)]
    outer += [(j, i) for i, j in outer]
    inner = [(i, i + 1) for i in range(0, owners, 2)]
    inner += [(j, i) for i, j in inner]
    tables = jnp.asarray(wave_tables(size))

    outer_places = lax.ppermute(positions, "lat", outer)
    inner_places = lax.ppermute(positions, "lat", inner)
    for_outer, for_inner = cut_rims(object_slab, outer_places, inner_places, size)
    from_outer = lax.ppermute(for_outer, "lat", outer)
    owns = cut_own(here, object_slab, positions, size)
    owns = shifted(owns)
    from_inner = lax.ppermute(for_inner, "lat", inner)
    control = steering(here, counts, positions, strip)
    left, right, start, measured = prepare(control, probe, intensity, tables)
    halos = blend(here, positions, from_outer, from_inner)
    halos = shifted(halos)

    *grad_owns, grad_halo = chain(control, owns, halos, left, right, start, measured)

    grad_halo = lax.all_to_all(grad_halo, "cuts", 0, 0, tiled=True)
    back_outer = lax.ppermute(grad_halo, "lat", outer)
    back_inner = lax.ppermute(grad_halo, "lat", inner)
    grad_owns, grad_halo = lax.optimization_barrier((grad_owns, grad_halo))
    grad_owns = shifted(grad_owns)
    rims = gather_rims(here, outer_places, inner_places, back_outer, back_inner, width)
    summed = gather_strip(here, positions, grad_owns, rims)
    return summed[:, None]


def solution(mesh):
    return jax.shard_map(
        strip_gradient,
        mesh=mesh,
        in_specs=(
            P(None, "cuts", "lat", None),
            P(),
            P("lat", None, None),
            P("lat", None),
            P("lat"),
        ),
        out_specs=P(None, "cuts", "lat", None),
        check_vma=False,
    )
```
